32 devices in a mesh: rep: 2 (over x), fsdp: 16 (over z, y, core).
Axes of the slice: x: 2, y: 2, z: 4, core: 2. Of those that a mesh axis runs over, the one named last changes fastest.
Arguments:
- tokens: bfloat16 [256, 128, 768], P(('rep', 'fsdp')), may hold values from -6 to 6
- timesteps: int32 [256], P(('rep', 'fsdp')), may hold values from 0 to 1999
- split_at: int32 [256], P(('rep', 'fsdp')), may hold values from 32 to 96
- sample_weight: float32 [256], P(('rep', 'fsdp')), may hold values from 0.5 to 2
- cotangent: bfloat16 [256, 128, 768], P(('rep', 'fsdp')), may hold values from -6 to 6
- time_w1: bfloat16 [128, 512], P('fsdp'), may hold values from -0.75 to 0.75
- time_w2: bfloat16 [512, 768], P('fsdp'), may hold values from -0.25 to 0.25
- attn_qkv: bfloat16 [768, 2304], P('fsdp'), may hold values from -0.21875 to 0.21875
- attn_out: bfloat16 [768, 768], P('fsdp'), may hold values from -0.875 to 0.875
- ff_in: bfloat16 [768, 3072], P('fsdp'), may hold values from -0.21875 to 0.21875
- ff_out: bfloat16 [3072, 768], P('fsdp'), may hold values from -0.109375 to 0.109375
- biases: bfloat16 [7, 768], P(None, 'fsdp'), may hold values from -3 to 3
- norm_gains: bfloat16 [2, 768], P(None, 'fsdp'), may hold values from 0.5 to 1.5
- ff_bias: bfloat16 [3072], P('fsdp'), may hold values from -3 to 3
- time_bias: bfloat16 [512], P('fsdp'), may hold values from -3 to 3
Outputs:
- output: bfloat16 [256, 128, 768], P(('rep', 'fsdp'))
- grad_tokens: bfloat16 [256, 128, 768], P(('rep', 'fsdp'))
- grad_time_w1: float32 [128, 512], P('fsdp')
- grad_time_w2: float32 [512, 768], P('fsdp')
- grad_attn_qkv: float32 [768, 2304], P('fsdp')
- grad_attn_out: float32 [768, 768], P('fsdp')
- grad_ff_in: float32 [768, 3072], P('fsdp')
- grad_ff_out: float32 [3072, 768], P('fsdp')
- grad_biases: float32 [7, 768], P(None, 'fsdp')
- grad_norm_gains: float32 [2, 768], P(None, 'fsdp')
- grad_ff_bias: float32 [3072], P('fsdp')
- grad_time_bias: float32 [512], P('fsdp')
The draws below stay inside these ranges and needn't reach their ends.
All inputs are finite; a program needn't handle non-finite values.
Results may differ from the reference program's by a relative error of at most 0.017.
Values may be sent and summed in bfloat16 or wider, within the bound.
No kernel may reach another device: no remote copies, remote signals or barrier semaphores. Data moves between devices by JAX's collectives and lax.ppermute only.
A program may use at most 192 MiB of HBM per device.

```python
import math
import jax
import jax.numpy as jnp
from jax import lax

D = 768
HEADS = 12
HEAD = 64
FF = 3072
TE = 128
TE_HID = 512
SEQ = 128
STEPS = 2000
SEQ_DEV = 8
SEQS = 256
N_REP = 2
N_FSDP = 16


def draw_timesteps(key, part):
    first_key, second_key, place_key, other_key = jax.random.split(jax.random.fold_in(key, 11), 4)
    first = jax.random.randint(first_key, (SEQS,), 0, STEPS)
    second = jax.random.randint(second_key, (SEQS,), 0, STEPS)
    steps_out = jnp.minimum(first, second).astype(jnp.int32)
    high_place = jax.random.randint(place_key, (), 0, SEQS).astype(jnp.int32)
    offset = jax.random.randint(other_key, (), 0, SEQS - 1).astype(jnp.int32)
    low_place = (high_place + 1 + offset) % SEQS
    places = jnp.arange(SEQS, dtype=jnp.int32)
    steps_out = jnp.where(places == high_place, STEPS - 1, steps_out)
    steps_out = jnp.where(places == low_place, 0, steps_out)
    return steps_out.astype(jnp.int32)


def place_ends(drawn, rng, low, top_value):
    spot = [jax.random.randint(jax.random.fold_in(rng, axis), (), 0, length) for axis, length in enumerate(drawn.shape)]
    widest = drawn.shape.index(max(drawn.shape))
    neighbour = spot[:widest] + [(spot[widest] + 1) % drawn.shape[widest]] + spot[widest + 1:]
    return drawn.at[tuple(spot)].set(low).at[tuple(neighbour)].set(top_value)


def block_levels(own_key, extent, shards, smallest, largest):
    factor_of = 1.0
    for position, blocks in shards:
        draws = jax.random.uniform(jax.random.fold_in(jax.random.fold_in(own_key, 6), position), (blocks,), jnp.float32, smallest / len(shards), largest / len(shards))
        factor_of = factor_of * jnp.repeat(jnp.exp(draws), extent[position] // blocks).reshape((-1,) + (1,) * (len(extent) - 1 - position))
    return factor_of


def scatter_about(own_key, extent, scale, most, cuts=(), kind=jnp.bfloat16):
    drawn = jax.random.normal(own_key, extent, jnp.float32) * scale
    if len(cuts) > 0:
        drawn = block_levels(own_key, extent, cuts, -0.22, 0.18) * drawn
    return jnp.clip(drawn, min=-most, max=most).astype(kind)


def setup_inputs(seed: int = 0) -> dict:
    streams_of = jax.random.split(jax.random.key(seed), 16)
    return {
        "tokens": scatter_about(streams_of[0], (SEQS, SEQ, D), 1.0, 6.0, ((0, 32),)),
        "timesteps": draw_timesteps(jax.random.fold_in(streams_of[15], 71), 0),
        "split_at": place_ends(jax.random.randint(streams_of[2], (SEQS,), SEQ // 4, 3 * SEQ // 4 + 1), jax.random.fold_in(streams_of[2], 1), SEQ // 4, (3 * SEQ // 4 + 1) - 1).astype(jnp.int32),
        "sample_weight": jnp.clip(jnp.exp(math.log(2.0) - 1.3862944 * jax.random.uniform(streams_of[3], (SEQS,), jnp.float32) ** block_levels(streams_of[3], (SEQS,), ((0, 32),), -0.2, 0.2)), 0.5, 2.0),
        "cotangent": scatter_about(streams_of[4], (SEQS, SEQ, D), 1.0, 6.0, ((0, 32),)),
        "time_w1": scatter_about(streams_of[5], (TE, TE_HID), (TE // 2) ** -0.5, 0.75, ((0, 16),)),
        "time_w2": scatter_about(streams_of[6], (TE_HID, D), TE_HID ** -0.5, 0.25, ((0, 16),)),
        "attn_qkv": scatter_about(streams_of[7], (D, 3 * D), D ** -0.5, 0.21875, ((0, 16),)),
        "attn_out": scatter_about(streams_of[8], (D, D), (D // 16) ** -0.5, 0.875, ((0, 16),)),
        "ff_in": scatter_about(streams_of[9], (D, FF), D ** -0.5, 0.21875, ((0, 16),)),
        "ff_out": scatter_about(streams_of[10], (FF, D), FF ** -0.5, 0.109375, ((0, 16),)),
        "biases": scatter_about(streams_of[11], (7, D), 0.5, 3.0, ((1, 16),)),
        "norm_gains": jnp.clip(1.0 + 0.1 * jax.random.normal(streams_of[12], (2, D), jnp.float32), 0.5, 1.5).astype(jnp.bfloat16),
        "ff_bias": scatter_about(streams_of[13], (FF,), 0.5, 3.0, ((0, 16),)),
        "time_bias": scatter_about(streams_of[14], (TE_HID,), 0.5, 3.0, ((0, 16),)),
    }


@jax.custom_vjp
def low(v):
    return lax.optimization_barrier(v.astype(jnp.bfloat16)).astype(jnp.float32)

@jax.custom_vjp
def low_back(v):
    return v

def low_keep(v):
    return (low(v), None)

def low_pass(kept, grad):
    return (grad,)

def back_keep(v):
    return (v, None)

def back_low(kept, grad):
    return (low(grad),)
low.defvjp(low_keep, low_pass)
low_back.defvjp(back_keep, back_low)

def precise(left, right):
    return jnp.dot(left, right, precision=lax.Precision.HIGHEST, preferred_element_type=jnp.float32)

def sinusoid(steps_in):
    half_width = TE // 2
    frequency = jnp.exp(-math.log(10000.0) * jnp.arange(half_width, dtype=jnp.float32) / half_width)
    angles = steps_in.astype(jnp.float32)[:, None] * frequency[None, :]
    return jnp.concatenate([jnp.cos(angles), jnp.sin(angles)], axis=1)

def normalize(values_in, gain_vec, shift_vec):
    center = lax.optimization_barrier(jnp.mean(values_in, axis=-1, keepdims=True))
    spread = lax.optimization_barrier(jnp.mean((values_in - center) ** 2, axis=-1, keepdims=True))
    return (values_in - center) * lax.rsqrt(spread + 1e-05) * gain_vec + shift_vec

def attention(projected):
    groups = projected.shape[0]
    heads_view = projected.reshape(groups, SEQ, 3, HEADS, HEAD)
    queries = heads_view[:, :, 0]
    key_heads = heads_view[:, :, 1]
    value_heads = heads_view[:, :, 2]
    raw_scores = low_back(jnp.einsum('glhe,gmhe->ghlm', queries, key_heads, precision=lax.Precision.HIGHEST))
    attend = jax.nn.softmax(raw_scores * 0.125, axis=-1)
    context = jnp.einsum('ghlm,gmhe->glhe', low(attend), value_heads, precision=lax.Precision.HIGHEST)
    return context.reshape(groups * SEQ, D)

def layer_forward(params, token_group, step_group):
    time_w1, time_w2, attn_qkv, attn_out, ff_in, ff_out, biases, norm_gains, ff_bias, time_bias = params
    groups = token_group.shape[0]
    sinus = sinusoid(step_group)
    pre_time = precise(sinus, time_w1) + time_bias
    temb = precise(jax.nn.silu(pre_time), time_w2) + biases[0]
    token_rows = (token_group + temb[:, None, :]).reshape(groups * SEQ, D)
    qkv_bias = jnp.concatenate([biases[1], jnp.zeros((D,), jnp.float32), biases[2]])
    projected = low(low_back(precise(low(token_rows), attn_qkv)) + qkv_bias)
    context = low(low_back(attention(projected.reshape(groups, SEQ, 3 * D))))
    resid_attn = token_rows + low_back(precise(context, attn_out)) + biases[3]
    normed = normalize(resid_attn, norm_gains[0], biases[4])
    ff_inner = low_back(precise(low(normed), ff_in)) + ff_bias
    active = low(jax.nn.gelu(ff_inner, approximate=False))
    resid_ff = normed + low_back(precise(active, ff_out)) + biases[5]
    output = normalize(resid_ff, norm_gains[1], biases[6])
    return output.reshape(groups, SEQ, D)

def reference(tokens, timesteps, split_at, sample_weight, cotangent, time_w1, time_w2, attn_qkv, attn_out, ff_in, ff_out, biases, norm_gains, ff_bias, time_bias):
    params = tuple((weight.astype(jnp.float32) for weight in (time_w1, time_w2, attn_qkv, attn_out, ff_in, ff_out, biases, norm_gains, ff_bias, time_bias)))
    groups = N_REP * N_FSDP
    token_groups = tokens.astype(jnp.float32).reshape(groups, SEQ_DEV, SEQ, D)
    step_groups = timesteps.reshape(groups, SEQ_DEV)
    split_groups = split_at.reshape(groups, SEQ_DEV)
    weight_groups = sample_weight.astype(jnp.float32).reshape(groups, SEQ_DEV)
    cot_groups = cotangent.astype(jnp.float32).reshape(groups, SEQ_DEV, SEQ, D)
    positions = jnp.arange(SEQ, dtype=jnp.int32)

    def group_step(totals, group_data):
        token_group, step_group, split_group, weight_group, cot_group = group_data
        target_mask = (positions[None, :] >= split_group[:, None]).astype(jnp.float32)
        grad_out = cot_group * (weight_group[:, None] * target_mask)[:, :, None]

        def closed(params_in, tokens_in):
            return layer_forward(params_in, tokens_in, step_group)
        output, pull_back = jax.vjp(closed, params, token_group)
        grads, grad_in = pull_back(grad_out)
        totals = tuple((total + grad for total, grad in zip(totals, grads)))
        return (totals, (output.astype(jnp.bfloat16), grad_in.astype(jnp.bfloat16)))
    start = tuple((jnp.zeros_like(weight) for weight in params))
    totals, (outputs, grad_ins) = lax.scan(group_step, start, (token_groups, step_groups, split_groups, weight_groups, cot_groups))
    output = outputs.reshape(SEQS, SEQ, D)
    grad_tokens = grad_ins.reshape(SEQS, SEQ, D)
    return (output, grad_tokens, totals[0], totals[1], totals[2], totals[3], totals[4], totals[5], totals[6], totals[7], totals[8], totals[9])
```

```python
import math

import jax
import jax.numpy as jnp
from jax import lax
from jax.sharding import PartitionSpec as P

HEADS = 12
HEAD = 64


def precise(left, right):
    return jnp.dot(left, right, precision=lax.Precision.HIGHEST, preferred_element_type=jnp.float32)


def sinusoid(steps_in, width):
    half_width = width // 2
    frequency = jnp.exp(-math.log(10000.0) * jnp.arange(half_width, dtype=jnp.float32) / half_width)
    angles = steps_in.astype(jnp.float32)[:, None] * frequency[None, :]
    return jnp.concatenate([jnp.cos(angles), jnp.sin(angles)], axis=1)


def normalize(values_in, gain_vec, shift_vec):
    center = jnp.mean(values_in, axis=-1, keepdims=True)
    spread = jnp.mean((values_in - center) ** 2, axis=-1, keepdims=True)
    return (values_in - center) * lax.rsqrt(spread + 1e-05) * gain_vec + shift_vec


def gelu_exact(values_in):
    return jax.nn.gelu(values_in, approximate=False)


def contract_rows(left, right):
    return lax.dot_general(
        left, right, (((0,), (0,)), ((), ())), preferred_element_type=jnp.float32
    )


def times_transpose(left, right):
    return lax.dot_general(
        left, right, (((1,), (1,)), ((), ())), preferred_element_type=jnp.float32
    )


def swap_bit(count, bit):
    return [(place, place ^ (1 << bit)) for place in range(count)]


def add_up(terms):
    total = terms[0].astype(jnp.float32)
    for term in terms[1:]:
        total = total + term.astype(jnp.float32)
    return total


def reduce_to_owner(blocks):
    count = lax.axis_size("fsdp")
    place = lax.axis_index("fsdp")
    terms = [blocks]
    left, bit = count, 0
    while left > 1:
        mine = (place >> bit) & 1
        paired = [term.reshape((left // 2, 2) + term.shape[1:]) for term in terms]
        away = [lax.dynamic_index_in_dim(term, 1 - mine, 1, keepdims=False) for term in paired]
        home = [lax.dynamic_index_in_dim(term, mine, 1, keepdims=False) for term in paired]
        sent = add_up(away).astype(jnp.bfloat16)
        terms = home + [lax.ppermute(sent, "fsdp", swap_bit(count, bit))]
        left, bit = left // 2, bit + 1
    return add_up(terms)[0]


def sum_replicas(share):
    replicas = lax.axis_size("rep")
    low = share.astype(jnp.bfloat16)
    if replicas == 1:
        return low.astype(jnp.float32)
    if replicas == 2:
        other = lax.ppermute(low, "rep", [(0, 1), (1, 0)])
        return low.astype(jnp.float32) + other.astype(jnp.float32)
    return lax.psum(low, "rep").astype(jnp.float32)


def reduce_matrix(grad):
    count = lax.axis_size("fsdp")
    blocks = grad.astype(jnp.bfloat16).reshape(count, grad.shape[0] // count, grad.shape[1])
    return sum_replicas(reduce_to_owner(blocks))


def reduce_small(time_w2_grad, parts):
    count = lax.axis_size("fsdp")
    width = time_w2_grad.shape[1]
    big = time_w2_grad.astype(jnp.bfloat16).reshape(count, -1, width)
    flat = jnp.concatenate([part.astype(jnp.bfloat16) for part in parts], axis=1)
    sizes = [part.shape[1] for part in parts]
    used = sum(sizes)
    rows = -(-used // width)
    flat = jnp.pad(flat, ((0, 0), (0, rows * width - used))).reshape(count, rows, width)
    summed = sum_replicas(reduce_to_owner(jnp.concatenate([big, flat], axis=1)))
    own_big = summed[: big.shape[1]]
    own_flat = summed[big.shape[1] :].reshape(-1)
    pieces, start = [], 0
    for size in sizes:
        pieces.append(own_flat[start : start + size])
        start += size
    return own_big, pieces


def per_device(
    tokens,
    timesteps,
    split_at,
    sample_weight,
    cotangent,
    time_w1,
    time_w2,
    attn_qkv,
    attn_out,
    ff_in,
    ff_out,
    biases,
    norm_gains,
    ff_bias,
    time_bias,
):
    seqs, length, width = tokens.shape
    gathered = (
        lax.all_gather(time_w1, "fsdp", axis=0, tiled=True),
        lax.all_gather(time_w2, "fsdp", axis=0, tiled=True),
        lax.all_gather(attn_qkv, "fsdp", axis=0, tiled=True),
        lax.all_gather(attn_out, "fsdp", axis=0, tiled=True),
        lax.all_gather(ff_in, "fsdp", axis=0, tiled=True),
        lax.all_gather(ff_out, "fsdp", axis=0, tiled=True),
        lax.all_gather(biases, "fsdp", axis=1, tiled=True),
        lax.all_gather(norm_gains, "fsdp", axis=1, tiled=True),
        lax.all_gather(ff_bias, "fsdp", axis=0, tiled=True),
        lax.all_gather(time_bias, "fsdp", axis=0, tiled=True),
    )
    (
        full_tw1,
        full_tw2,
        full_qkv,
        full_out,
        full_in,
        full_down,
        full_bias,
        full_gain,
        full_ffb,
        full_tb,
    ) = gathered
    bias_rows = full_bias.astype(jnp.float32)
    gain_rows = full_gain.astype(jnp.float32)
    sinus = sinusoid(timesteps, full_tw1.shape[0])
    pre_time = precise(sinus, full_tw1.astype(jnp.float32)) + full_tb.astype(jnp.float32)
    hidden_time, silu_pull = jax.vjp(jax.nn.silu, pre_time)
    temb = precise(hidden_time, full_tw2.astype(jnp.float32)) + bias_rows[0]
    token_rows = (tokens.astype(jnp.float32) + temb[:, None, :]).reshape(seqs * length, width)
    rows_low = token_rows.astype(jnp.bfloat16)
    qkv_bias = jnp.concatenate([bias_rows[1], jnp.zeros((width,), jnp.float32), bias_rows[2]])
    projected = (jnp.dot(rows_low, full_qkv, preferred_element_type=jnp.float32) + qkv_bias).astype(
        jnp.bfloat16
    )
    heads_view = projected.reshape(seqs, length, 3, HEADS, HEAD)
    queries = heads_view[:, :, 0]
    key_heads = heads_view[:, :, 1]
    value_heads = heads_view[:, :, 2]
    raw_scores = jnp.einsum(
        "slhe,smhe->shlm", queries, key_heads, preferred_element_type=jnp.float32
    )
    attend = jax.nn.softmax(raw_scores * 0.125, axis=-1)
    attend_low = attend.astype(jnp.bfloat16)
    context = jnp.einsum(
        "shlm,smhe->slhe", attend_low, value_heads, preferred_element_type=jnp.float32
    )
    context_low = context.reshape(seqs * length, width).astype(jnp.bfloat16)
    resid_attn = (
        token_rows
        + jnp.dot(context_low, full_out, preferred_element_type=jnp.float32)
        + bias_rows[3]
    )
    normed, first_pull = jax.vjp(normalize, resid_attn, gain_rows[0], bias_rows[4])
    normed_low = normed.astype(jnp.bfloat16)
    ff_inner = jnp.dot(normed_low, full_in, preferred_element_type=jnp.float32) + full_ffb.astype(
        jnp.float32
    )
    active, gelu_pull = jax.vjp(gelu_exact, ff_inner)
    active_low = active.astype(jnp.bfloat16)
    resid_ff = (
        normed + jnp.dot(active_low, full_down, preferred_element_type=jnp.float32) + bias_rows[5]
    )
    output, second_pull = jax.vjp(normalize, resid_ff, gain_rows[1], bias_rows[6])
    back_tw2, back_qkv, back_out, back_in, back_down = (
        lax.all_gather(time_w2, "fsdp", axis=0, tiled=True),
        lax.all_gather(attn_qkv, "fsdp", axis=0, tiled=True),
        lax.all_gather(attn_out, "fsdp", axis=0, tiled=True),
        lax.all_gather(ff_in, "fsdp", axis=0, tiled=True),
        lax.all_gather(ff_out, "fsdp", axis=0, tiled=True),
    )
    positions = lax.iota(jnp.int32, length)
    target_mask = (positions[None, :] >= split_at[:, None]).astype(jnp.float32)
    grad_out = (
        cotangent.astype(jnp.float32) * (sample_weight[:, None] * target_mask)[:, :, None]
    ).reshape(seqs * length, width)
    d_ff, d_gain_two, d_shift_two = second_pull(grad_out)
    d_ffout_bias = jnp.sum(d_ff, axis=0)
    d_ff_low = d_ff.astype(jnp.bfloat16)
    grad_down = contract_rows(active_low, d_ff_low)
    d_active = times_transpose(d_ff_low, back_down)
    (d_inner,) = gelu_pull(d_active)
    d_ff_bias = jnp.sum(d_inner, axis=0)
    d_inner_low = d_inner.astype(jnp.bfloat16)
    grad_in = contract_rows(normed_low, d_inner_low)
    d_normed = d_ff + times_transpose(d_inner_low, back_in)
    d_attn, d_gain_one, d_shift_one = first_pull(d_normed)
    d_out_bias = jnp.sum(d_attn, axis=0)
    d_attn_low = d_attn.astype(jnp.bfloat16)
    grad_out_proj = contract_rows(context_low, d_attn_low)
    d_context = (
        times_transpose(d_attn_low, back_out)
        .astype(jnp.bfloat16)
        .reshape(seqs, length, HEADS, HEAD)
    )
    d_attend = jnp.einsum(
        "slhe,smhe->shlm", d_context, value_heads, preferred_element_type=jnp.float32
    )
    d_values = jnp.einsum(
        "shlm,slhe->smhe", attend_low, d_context, preferred_element_type=jnp.float32
    )
    d_scores = attend * (d_attend - jnp.sum(attend * d_attend, axis=-1, keepdims=True))
    d_raw = (d_scores * 0.125).astype(jnp.bfloat16)
    d_queries = jnp.einsum("shlm,smhe->slhe", d_raw, key_heads, preferred_element_type=jnp.float32)
    d_keys = jnp.einsum("shlm,slhe->smhe", d_raw, queries, preferred_element_type=jnp.float32)
    d_projected = jnp.stack([d_queries, d_keys, d_values], axis=2).reshape(seqs * length, 3 * width)
    d_query_bias = jnp.sum(d_queries, axis=(0, 1)).reshape(width)
    d_value_bias = jnp.sum(d_values, axis=(0, 1)).reshape(width)
    d_projected_low = d_projected.astype(jnp.bfloat16)
    grad_qkv = contract_rows(rows_low, d_projected_low)
    d_rows = d_attn + times_transpose(d_projected_low, back_qkv)
    d_rows_seq = d_rows.reshape(seqs, length, width)
    d_temb = jnp.sum(d_rows_seq, axis=1)
    d_temb_bias = jnp.sum(d_temb, axis=0)
    grad_tw2 = precise(hidden_time.T, d_temb)
    d_hidden_time = precise(d_temb, back_tw2.astype(jnp.float32).T)
    (d_pre_time,) = silu_pull(d_hidden_time)
    d_time_bias = jnp.sum(d_pre_time, axis=0)
    grad_tw1 = precise(sinus.T, d_pre_time)
    grad_bias_rows = jnp.stack(
        [
            d_temb_bias,
            d_query_bias,
            d_value_bias,
            d_out_bias,
            d_shift_one,
            d_ffout_bias,
            d_shift_two,
        ]
    )
    grad_gain_rows = jnp.stack([d_gain_one, d_gain_two])
    count = lax.axis_size("fsdp")

    def by_column(rows_in):
        rows_n, cols_n = rows_in.shape
        return rows_in.reshape(rows_n, count, cols_n // count).swapaxes(0, 1).reshape(count, -1)

    share_down = reduce_matrix(grad_down)
    share_in = reduce_matrix(grad_in)
    share_out = reduce_matrix(grad_out_proj)
    share_qkv = reduce_matrix(grad_qkv)
    share_tw2, pieces = reduce_small(
        grad_tw2,
        [
            grad_tw1.reshape(count, -1),
            by_column(grad_bias_rows),
            by_column(grad_gain_rows),
            d_ff_bias.reshape(count, -1),
            d_time_bias.reshape(count, -1),
        ],
    )
    summed = (
        pieces[0].reshape(time_w1.shape),
        share_tw2,
        share_qkv,
        share_out,
        share_in,
        share_down,
        pieces[1].reshape(biases.shape),
        pieces[2].reshape(norm_gains.shape),
        pieces[3],
        pieces[4],
    )
    output_low = output.reshape(seqs, length, width).astype(jnp.bfloat16)
    grad_tokens = d_rows_seq.astype(jnp.bfloat16)
    return (
        output_low,
        grad_tokens,
        summed[0],
        summed[1],
        summed[2],
        summed[3],
        summed[4],
        summed[5],
        summed[6],
        summed[7],
        summed[8],
        summed[9],
    )


def solution(mesh):
    placed = (
        P(("rep", "fsdp"), None, None),
        P(("rep", "fsdp")),
        P(("rep", "fsdp")),
        P(("rep", "fsdp")),
        P(("rep", "fsdp"), None, None),
        P("fsdp", None),
        P("fsdp", None),
        P("fsdp", None),
        P("fsdp", None),
        P("fsdp", None),
        P("fsdp", None),
        P(None, "fsdp"),
        P(None, "fsdp"),
        P("fsdp"),
        P("fsdp"),
    )
    return jax.shard_map(
        per_device,
        mesh=mesh,
        in_specs=placed,
        out_specs=(
            P(("rep", "fsdp"), None, None),
            P(("rep", "fsdp"), None, None),
            P("fsdp", None),
            P("fsdp", None),
            P("fsdp", None),
            P("fsdp", None),
            P("fsdp", None),
            P("fsdp", None),
            P(None, "fsdp"),
            P(None, "fsdp"),
            P("fsdp"),
            P("fsdp"),
        ),
        check_vma=False,
    )
```

```python
import math

import jax
import jax.numpy as jnp
from jax import lax
from jax.experimental import pallas as pl
from jax.sharding import PartitionSpec as P


HEAD = 64


def precise(left, right):
    return jnp.dot(left, right, precision=lax.Precision.HIGHEST, preferred_element_type=jnp.float32)


def sinusoid(steps_in, width):
    half_width = width // 2
    frequency = jnp.exp(-math.log(10000.0) * jnp.arange(half_width, dtype=jnp.float32) / half_width)
    angles = steps_in.astype(jnp.float32)[:, None] * frequency[None, :]
    return jnp.concatenate([jnp.cos(angles), jnp.sin(angles)], axis=1)


def normalize(values_in, gain_vec, shift_vec):
    center = jnp.mean(values_in, axis=-1, keepdims=True)
    spread = jnp.mean((values_in - center) ** 2, axis=-1, keepdims=True)
    return (values_in - center) * lax.rsqrt(spread + 1e-05) * gain_vec + shift_vec


def contract_rows(left, right):
    return lax.dot_general(
        left, right, (((0,), (0,)), ((), ())), preferred_element_type=jnp.float32
    )


def times_transpose(left, right):
    return lax.dot_general(
        left, right, (((1,), (1,)), ((), ())), preferred_element_type=jnp.float32
    )


def low_dot(left, right, dims):
    return lax.dot_general(left, right, (dims, ((), ())), preferred_element_type=jnp.float32)


def two_heads(block):
    first = lax.broadcasted_iota(jnp.int32, block.shape, 1) < HEAD
    zero = jnp.zeros_like(block)
    return jnp.concatenate([jnp.where(first, block, zero), jnp.where(first, zero, block)], axis=0)


def attend_forward_body(projected_ref, context_ref, attend_ref):
    length, width = context_ref.shape
    pair = 2 * HEAD
    for start in range(0, width, pair):
        queries = projected_ref[:, start : start + pair] * 0.125
        keys = two_heads(projected_ref[:, width + start : width + start + pair])
        values = two_heads(projected_ref[:, 2 * width + start : 2 * width + start + pair])
        scores = low_dot(queries, keys, ((1,), (1,)))
        parts = []
        for half in range(2):
            part = scores[:, half * length : (half + 1) * length]
            part = jnp.exp(part - jnp.max(part, axis=1, keepdims=True))
            parts.append(part * (1.0 / jnp.sum(part, axis=1, keepdims=True)))
        attend = jnp.concatenate(parts, axis=1).astype(jnp.bfloat16)
        context = low_dot(attend, values, ((1,), (0,)))
        context_ref[:, start : start + pair] = context.astype(jnp.bfloat16)
        at = start // HEAD * length
        attend_ref[:, at : at + 2 * length] = attend


def attend_forward(projected, length):
    rows, wide = projected.shape
    width = wide // 3
    kept = width // HEAD * length
    return pl.pallas_call(
        attend_forward_body,
        grid=(rows // length,),
        in_specs=[pl.BlockSpec((length, wide), lambda seq: (seq, 0))],
        out_specs=[
            pl.BlockSpec((length, width), lambda seq: (seq, 0)),
            pl.BlockSpec((length, kept), lambda seq: (seq, 0)),
        ],
        out_shape=[
            jax.ShapeDtypeStruct((rows, width), jnp.bfloat16),
            jax.ShapeDtypeStruct((rows, kept), jnp.bfloat16),
        ],
        name="attend_forward",
    )(projected)


def attend_backward_body(projected_ref, attend_ref, d_context_ref, d_projected_ref, sums_ref):
    length, width = d_context_ref.shape
    pair = 2 * HEAD
    first = lax.broadcasted_iota(jnp.int32, (length, pair), 1) < HEAD
    for start in range(0, width, pair):
        cols = [slice(part * width + start, part * width + start + pair) for part in range(3)]
        queries = projected_ref[:, cols[0]] * 0.125
        keys = two_heads(projected_ref[:, cols[1]] * 0.125)
        values = two_heads(projected_ref[:, cols[2]])
        d_context = d_context_ref[:, start : start + pair]
        at = start // HEAD * length
        attend = attend_ref[:, at : at + 2 * length]
        d_attend = low_dot(d_context, values, ((1,), (1,)))
        raw = []
        for half in range(2):
            place = slice(half * length, (half + 1) * length)
            weights = attend[:, place].astype(jnp.float32)
            slopes = d_attend[:, place]
            total = jnp.sum(weights * slopes, axis=1, keepdims=True)
            raw.append(weights * (slopes - total))
        d_raw = jnp.concatenate(raw, axis=1).astype(jnp.bfloat16)
        d_queries = low_dot(d_raw, keys, ((1,), (0,)))
        both_keys = low_dot(d_raw, queries, ((0,), (0,)))
        both_values = low_dot(attend, d_context, ((0,), (0,)))
        d_keys = jnp.where(first, both_keys[:length], both_keys[length:])
        d_values = jnp.where(first, both_values[:length], both_values[length:])
        d_projected_ref[:, cols[0]] = d_queries.astype(jnp.bfloat16)
        d_projected_ref[:, cols[1]] = d_keys.astype(jnp.bfloat16)
        d_projected_ref[:, cols[2]] = d_values.astype(jnp.bfloat16)
        sums_ref[0, 0:1, start : start + pair] = jnp.sum(d_queries, axis=0, keepdims=True)
        sums_ref[0, 1:2, start : start + pair] = jnp.sum(d_values, axis=0, keepdims=True)


def attend_backward(projected, attend, d_context, length):
    rows, wide = projected.shape
    width = wide // 3
    seqs = rows // length
    return pl.pallas_call(
        attend_backward_body,
        grid=(seqs,),
        in_specs=[
            pl.BlockSpec((length, wide), lambda seq: (seq, 0)),
            pl.BlockSpec((length, attend.shape[1]), lambda seq: (seq, 0)),
            pl.BlockSpec((length, width), lambda seq: (seq, 0)),
        ],
        out_specs=[
            pl.BlockSpec((length, wide), lambda seq: (seq, 0)),
            pl.BlockSpec((1, 2, width), lambda seq: (seq, 0, 0)),
        ],
        out_shape=[
            jax.ShapeDtypeStruct((rows, wide), jnp.bfloat16),
            jax.ShapeDtypeStruct((seqs, 2, width), jnp.float32),
        ],
        name="attend_backward",
    )(projected, attend, d_context)


def swap_bit(count, bit):
    return [(place, place ^ (1 << bit)) for place in range(count)]


def add_up(terms):
    total = terms[0].astype(jnp.float32)
    for term in terms[1:]:
        total = total + term.astype(jnp.float32)
    return total


def reduce_stages(blocks, rep_first):
    count = lax.axis_size("fsdp")
    place = lax.axis_index("fsdp")
    replica = lax.axis_index("rep")
    cross = [(0, 1), (1, 0)]
    half = blocks.shape[-1] // 2
    terms = [blocks]
    left, bit = count, 0
    while left > 1:
        mine = (place >> bit) & 1
        paired = [term.reshape((left // 2, 2) + term.shape[1:]) for term in terms]
        away = [lax.dynamic_index_in_dim(term, 1 - mine, 1, keepdims=False) for term in paired]
        home = [lax.dynamic_index_in_dim(term, mine, 1, keepdims=False) for term in paired]
        sent = add_up(away).astype(jnp.bfloat16)
        terms = home + [lax.ppermute(sent, "fsdp", swap_bit(count, bit))]
        left, bit = left // 2, bit + 1
        if rep_first and bit == 1:
            away = [lax.dynamic_slice_in_dim(term, (1 - replica) * half, half, 2) for term in terms]
            home = [lax.dynamic_slice_in_dim(term, replica * half, half, 2) for term in terms]
            sent = add_up(away).astype(jnp.bfloat16)
            terms = home + [lax.ppermute(sent, "rep", cross)]
    low = add_up(terms)[0].astype(jnp.bfloat16)
    if lax.axis_size("rep") != 2:
        return lax.psum(low, "rep").astype(jnp.float32)
    other = lax.ppermute(low, "rep", cross)
    if not rep_first:
        return low.astype(jnp.float32) + other.astype(jnp.float32)
    pair = [jnp.where(replica == 0, low, other), jnp.where(replica == 0, other, low)]
    return jnp.concatenate(pair, axis=-1).astype(jnp.float32)


def reduce_matrix(grad, rep_first=False):
    count = lax.axis_size("fsdp")
    blocks = grad.astype(jnp.bfloat16).reshape(count, grad.shape[0] // count, grad.shape[1])
    return reduce_stages(blocks, rep_first and lax.axis_size("rep") == 2)


def reduce_small(time_w2_grad, parts):
    count = lax.axis_size("fsdp")
    width = time_w2_grad.shape[1]
    big = time_w2_grad.astype(jnp.bfloat16).reshape(count, -1, width)
    flat = jnp.concatenate([part.astype(jnp.bfloat16) for part in parts], axis=1)
    sizes = [part.shape[1] for part in parts]
    used = sum(sizes)
    rows = -(-used // width)
    flat = jnp.pad(flat, ((0, 0), (0, rows * width - used))).reshape(count, rows, width)
    summed = reduce_stages(jnp.concatenate([big, flat], axis=1), False)
    own_big = summed[: big.shape[1]]
    own_flat = summed[big.shape[1] :].reshape(-1)
    pieces, start = [], 0
    for size in sizes:
        pieces.append(own_flat[start : start + size])
        start += size
    return own_big, pieces


def gather_blocks(shard):
    count = lax.axis_size("fsdp")
    place = lax.axis_index("fsdp")
    held = shard[None]
    for bit in reversed(range(count.bit_length() - 1)):
        other = lax.ppermute(held, "fsdp", swap_bit(count, bit))
        upper = ((place >> bit) & 1) == 1
        pair = [jnp.where(upper, other, held), jnp.where(upper, held, other)]
        held = jnp.stack(pair, axis=1).reshape((2 * held.shape[0],) + held.shape[1:])
    return held


def gather_small(time_w2, parts):
    count = lax.axis_size("fsdp")
    width = time_w2.shape[1]
    flat = jnp.concatenate([part.reshape(-1) for part in parts])
    rows = -(-flat.shape[0] // width)
    flat = jnp.pad(flat, (0, rows * width - flat.shape[0])).reshape(rows, width)
    whole = gather_blocks(jnp.concatenate([time_w2, flat], axis=0))
    full_tw2 = whole[:, : time_w2.shape[0]].reshape(-1, width)
    flat = whole[:, time_w2.shape[0] :].reshape(count, -1)
    pieces, start = [], 0
    for part in parts:
        pieces.append(flat[:, start : start + part.size].reshape((count,) + part.shape))
        start += part.size
    return full_tw2, pieces


def per_device(
    tokens,
    timesteps,
    split_at,
    sample_weight,
    cotangent,
    time_w1,
    time_w2,
    attn_qkv,
    attn_out,
    ff_in,
    ff_out,
    biases,
    norm_gains,
    ff_bias,
    time_bias,
):
    seqs, length, width = tokens.shape
    width_in = attn_qkv.shape[1]
    full_tw2, pieces = gather_small(time_w2, [time_w1, biases, norm_gains, ff_bias, time_bias])
    full_tw1 = pieces[0].reshape(-1, time_w1.shape[1])
    full_bias = pieces[1].swapaxes(0, 1).reshape(biases.shape[0], -1)
    full_gain = pieces[2].swapaxes(0, 1).reshape(norm_gains.shape[0], -1)
    full_ffb = pieces[3].reshape(-1)
    full_tb = pieces[4].reshape(-1)
    full_qkv = gather_blocks(attn_qkv).reshape(-1, width_in)
    full_out = gather_blocks(attn_out).reshape(-1, attn_out.shape[1])
    full_in = gather_blocks(ff_in).reshape(-1, ff_in.shape[1])
    full_down = gather_blocks(ff_out).reshape(-1, ff_out.shape[1])
    bias_rows = full_bias.astype(jnp.float32)
    gain_rows = full_gain.astype(jnp.float32)
    sinus = sinusoid(timesteps, full_tw1.shape[0])
    pre_time = precise(sinus, full_tw1.astype(jnp.float32)) + full_tb.astype(jnp.float32)
    hidden_time, silu_pull = jax.vjp(jax.nn.silu, pre_time)
    temb = precise(hidden_time, full_tw2.astype(jnp.float32)) + bias_rows[0]
    token_rows = (tokens.astype(jnp.float32) + temb[:, None, :]).reshape(seqs * length, width)
    rows_low = token_rows.astype(jnp.bfloat16)
    qkv_bias = jnp.concatenate([bias_rows[1], jnp.zeros((width,), jnp.float32), bias_rows[2]])
    projected = jnp.dot(rows_low, full_qkv, preferred_element_type=jnp.float32) + qkv_bias
    projected = projected.astype(jnp.bfloat16)
    context_low, attend = attend_forward(projected, length)
    resid_attn = (
        token_rows
        + jnp.dot(context_low, full_out, preferred_element_type=jnp.float32)
        + bias_rows[3]
    )
    normed, first_pull = jax.vjp(normalize, resid_attn, gain_rows[0], bias_rows[4])
    normed_low = normed.astype(jnp.bfloat16)
    ff_inner = jnp.dot(normed_low, full_in, preferred_element_type=jnp.float32) + full_ffb.astype(
        jnp.float32
    )
    twice_cdf = 1.0 + lax.erf(ff_inner * math.sqrt(0.5))
    active_low = (0.5 * ff_inner * twice_cdf).astype(jnp.bfloat16)
    density = jnp.exp(-0.5 * ff_inner * ff_inner) * (1.0 / math.sqrt(2.0 * math.pi))
    slope_low = (0.5 * twice_cdf + ff_inner * density).astype(jnp.bfloat16)
    resid_ff = (
        normed + jnp.dot(active_low, full_down, preferred_element_type=jnp.float32) + bias_rows[5]
    )
    output, second_pull = jax.vjp(normalize, resid_ff, gain_rows[1], bias_rows[6])
    positions = lax.iota(jnp.int32, length)
    target_mask = (positions[None, :] >= split_at[:, None]).astype(jnp.float32)
    grad_out = (
        cotangent.astype(jnp.float32) * (sample_weight[:, None] * target_mask)[:, :, None]
    ).reshape(seqs * length, width)
    d_ff, d_gain_two, d_shift_two = second_pull(grad_out)
    d_ffout_bias = jnp.sum(d_ff, axis=0)
    d_ff_low = d_ff.astype(jnp.bfloat16)
    grad_down = contract_rows(active_low, d_ff_low)
    d_active = times_transpose(d_ff_low, full_down)
    d_inner = d_active * slope_low.astype(jnp.float32)
    d_ff_bias = jnp.sum(d_inner, axis=0)
    d_inner_low = d_inner.astype(jnp.bfloat16)
    grad_in = contract_rows(normed_low, d_inner_low)
    d_normed = d_ff + times_transpose(d_inner_low, full_in)
    d_attn, d_gain_one, d_shift_one = first_pull(d_normed)
    d_out_bias = jnp.sum(d_attn, axis=0)
    d_attn_low = d_attn.astype(jnp.bfloat16)
    grad_out_proj = contract_rows(context_low, d_attn_low)
    d_context = times_transpose(d_attn_low, full_out).astype(jnp.bfloat16)
    d_projected_low, bias_sums = attend_backward(projected, attend, d_context, length)
    bias_sums = jnp.sum(bias_sums, axis=0)
    d_query_bias, d_value_bias = bias_sums[0], bias_sums[1]
    grad_qkv = contract_rows(rows_low, d_projected_low)
    d_rows = d_attn + times_transpose(d_projected_low, full_qkv)
    d_rows_seq = d_rows.reshape(seqs, length, width)
    d_temb = jnp.sum(d_rows_seq, axis=1)
    d_temb_bias = jnp.sum(d_temb, axis=0)
    grad_tw2 = precise(hidden_time.T, d_temb)
    d_hidden_time = precise(d_temb, full_tw2.astype(jnp.float32).T)
    (d_pre_time,) = silu_pull(d_hidden_time)
    d_time_bias = jnp.sum(d_pre_time, axis=0)
    grad_tw1 = precise(sinus.T, d_pre_time)
    grad_bias_rows = jnp.stack(
        [
            d_temb_bias,
            d_query_bias,
            d_value_bias,
            d_out_bias,
            d_shift_one,
            d_ffout_bias,
            d_shift_two,
        ]
    )
    grad_gain_rows = jnp.stack([d_gain_one, d_gain_two])
    count = lax.axis_size("fsdp")

    def by_column(rows_in):
        rows_n, cols_n = rows_in.shape
        return rows_in.reshape(rows_n, count, cols_n // count).swapaxes(0, 1).reshape(count, -1)

    share_down = reduce_matrix(grad_down)
    share_in = reduce_matrix(grad_in, rep_first=True)
    share_out = reduce_matrix(grad_out_proj)
    middle = grad_qkv.shape[1] // 2
    share_qkv = jnp.concatenate(
        [reduce_matrix(grad_qkv[:, :middle]), reduce_matrix(grad_qkv[:, middle:], rep_first=True)],
        axis=1,
    )
    share_tw2, pieces = reduce_small(
        grad_tw2,
        [
            grad_tw1.reshape(count, -1),
            by_column(grad_bias_rows),
            by_column(grad_gain_rows),
            d_ff_bias.reshape(count, -1),
            d_time_bias.reshape(count, -1),
        ],
    )
    summed = (
        pieces[0].reshape(time_w1.shape),
        share_tw2,
        share_qkv,
        share_out,
        share_in,
        share_down,
        pieces[1].reshape(biases.shape),
        pieces[2].reshape(norm_gains.shape),
        pieces[3],
        pieces[4],
    )
    output_low = output.reshape(seqs, length, width).astype(jnp.bfloat16)
    grad_tokens = d_rows_seq.astype(jnp.bfloat16)
    return (
        output_low,
        grad_tokens,
        summed[0],
        summed[1],
        summed[2],
        summed[3],
        summed[4],
        summed[5],
        summed[6],
        summed[7],
        summed[8],
        summed[9],
    )


def solution(mesh):
    placed = (
        P(("rep", "fsdp"), None, None),
        P(("rep", "fsdp")),
        P(("rep", "fsdp")),
        P(("rep", "fsdp")),
        P(("rep", "fsdp"), None, None),
        P("fsdp", None),
        P("fsdp", None),
        P("fsdp", None),
        P("fsdp", None),
        P("fsdp", None),
        P("fsdp", None),
        P(None, "fsdp"),
        P(None, "fsdp"),
        P("fsdp"),
        P("fsdp"),
    )
    return jax.shard_map(
        per_device,
        mesh=mesh,
        in_specs=placed,
        out_specs=(
            P(("rep", "fsdp"), None, None),
            P(("rep", "fsdp"), None, None),
            P("fsdp", None),
            P("fsdp", None),
            P("fsdp", None),
            P("fsdp", None),
            P("fsdp", None),
            P("fsdp", None),
            P(None, "fsdp"),
            P(None, "fsdp"),
            P("fsdp"),
            P("fsdp"),
        ),
        check_vma=False,
    )
```

```python
import math

import jax
import jax.numpy as jnp
from jax import lax
from jax.experimental import pallas as pl
from jax.sharding import PartitionSpec as P


HEAD = 64


def precise(left, right):
    return jnp.dot(left, right, precision=lax.Precision.HIGHEST, preferred_element_type=jnp.float32)


def sinusoid(steps_in, width):
    half_width = width // 2
    frequency = jnp.exp(-math.log(10000.0) * jnp.arange(half_width, dtype=jnp.float32) / half_width)
    angles = steps_in.astype(jnp.float32)[:, None] * frequency[None, :]
    return jnp.concatenate([jnp.cos(angles), jnp.sin(angles)], axis=1)


def normalize(values_in, gain_vec, shift_vec):
    center = jnp.mean(values_in, axis=-1, keepdims=True)
    spread = jnp.mean((values_in - center) ** 2, axis=-1, keepdims=True)
    return (values_in - center) * lax.rsqrt(spread + 1e-05) * gain_vec + shift_vec


def contract_rows(left, right):
    return lax.dot_general(
        left, right, (((0,), (0,)), ((), ())), preferred_element_type=jnp.float32
    )


def times_transpose(left, right):
    return lax.dot_general(
        left, right, (((1,), (1,)), ((), ())), preferred_element_type=jnp.float32
    )


def low_dot(left, right, dims):
    return lax.dot_general(left, right, (dims, ((), ())), preferred_element_type=jnp.float32)


def two_heads(block):
    first = lax.broadcasted_iota(jnp.int32, block.shape, 1) < HEAD
    zero = jnp.zeros_like(block)
    return jnp.concatenate([jnp.where(first, block, zero), jnp.where(first, zero, block)], axis=0)


def attend_forward_body(projected_ref, context_ref, attend_ref):
    length, width = context_ref.shape
    pair = 2 * HEAD
    for start in range(0, width, pair):
        queries = projected_ref[:, start : start + pair] * 0.125
        keys = two_heads(projected_ref[:, width + start : width + start + pair])
        values = two_heads(projected_ref[:, 2 * width + start : 2 * width + start + pair])
        scores = low_dot(queries, keys, ((1,), (1,)))
        parts = []
        for half in range(2):
            part = scores[:, half * length : (half + 1) * length]
            part = jnp.exp(part - jnp.max(part, axis=1, keepdims=True))
            parts.append(part * (1.0 / jnp.sum(part, axis=1, keepdims=True)))
        attend = jnp.concatenate(parts, axis=1).astype(jnp.bfloat16)
        context = low_dot(attend, values, ((1,), (0,)))
        context_ref[:, start : start + pair] = context.astype(jnp.bfloat16)
        at = start // HEAD * length
        attend_ref[:, at : at + 2 * length] = attend


def attend_forward(projected, length):
    rows, wide = projected.shape
    width = wide // 3
    kept = width // HEAD * length
    return pl.pallas_call(
        attend_forward_body,
        grid=(rows // length,),
        in_specs=[pl.BlockSpec((length, wide), lambda seq: (seq, 0))],
        out_specs=[
            pl.BlockSpec((length, width), lambda seq: (seq, 0)),
            pl.BlockSpec((length, kept), lambda seq: (seq, 0)),
        ],
        out_shape=[
            jax.ShapeDtypeStruct((rows, width), jnp.bfloat16),
            jax.ShapeDtypeStruct((rows, kept), jnp.bfloat16),
        ],
        name="attend_forward",
    )(projected)


def attend_backward_body(projected_ref, attend_ref, d_context_ref, d_projected_ref, sums_ref):
    length, width = d_context_ref.shape
    pair = 2 * HEAD
    first = lax.broadcasted_iota(jnp.int32, (length, pair), 1) < HEAD
    for start in range(0, width, pair):
        cols = [slice(part * width + start, part * width + start + pair) for part in range(3)]
        queries = projected_ref[:, cols[0]] * 0.125
        keys = two_heads(projected_ref[:, cols[1]] * 0.125)
        values = two_heads(projected_ref[:, cols[2]])
        d_context = d_context_ref[:, start : start + pair]
        at = start // HEAD * length
        attend = attend_ref[:, at : at + 2 * length]
        d_attend = low_dot(d_context, values, ((1,), (1,)))
        raw = []
        for half in range(2):
            place = slice(half * length, (half + 1) * length)
            weights = attend[:, place].astype(jnp.float32)
            slopes = d_attend[:, place]
            total = jnp.sum(weights * slopes, axis=1, keepdims=True)
            raw.append(weights * (slopes - total))
        d_raw = jnp.concatenate(raw, axis=1).astype(jnp.bfloat16)
        d_queries = low_dot(d_raw, keys, ((1,), (0,)))
        both_keys = low_dot(d_raw, queries, ((0,), (0,)))
        both_values = low_dot(attend, d_context, ((0,), (0,)))
        d_keys = jnp.where(first, both_keys[:length], both_keys[length:])
        d_values = jnp.where(first, both_values[:length], both_values[length:])
        d_projected_ref[:, cols[0]] = d_queries.astype(jnp.bfloat16)
        d_projected_ref[:, cols[1]] = d_keys.astype(jnp.bfloat16)
        d_projected_ref[:, cols[2]] = d_values.astype(jnp.bfloat16)
        sums_ref[0, 0:1, start : start + pair] = jnp.sum(d_queries, axis=0, keepdims=True)
        sums_ref[0, 1:2, start : start + pair] = jnp.sum(d_values, axis=0, keepdims=True)


def attend_backward(projected, attend, d_context, length):
    rows, wide = projected.shape
    width = wide // 3
    seqs = rows // length
    return pl.pallas_call(
        attend_backward_body,
        grid=(seqs,),
        in_specs=[
            pl.BlockSpec((length, wide), lambda seq: (seq, 0)),
            pl.BlockSpec((length, attend.shape[1]), lambda seq: (seq, 0)),
            pl.BlockSpec((length, width), lambda seq: (seq, 0)),
        ],
        out_specs=[
            pl.BlockSpec((length, wide), lambda seq: (seq, 0)),
            pl.BlockSpec((1, 2, width), lambda seq: (seq, 0, 0)),
        ],
        out_shape=[
            jax.ShapeDtypeStruct((rows, wide), jnp.bfloat16),
            jax.ShapeDtypeStruct((seqs, 2, width), jnp.float32),
        ],
        name="attend_backward",
    )(projected, attend, d_context)


def inner_backward_body(
    d_out_ref, normed_ref, slope_ref, down_ref, in_ref,
    grad_in_ref, bias_ref, d_normed_ref,
):
    d_out = d_out_ref[...]
    d_inner = low_dot(d_out, down_ref[...], ((1,), (1,))) * slope_ref[...].astype(jnp.float32)
    bias_ref[...] = jnp.sum(d_inner, axis=0, keepdims=True)
    d_inner = d_inner.astype(jnp.bfloat16)
    grad_in_ref[...] = low_dot(normed_ref[...], d_inner, ((0,), (0,))).astype(jnp.bfloat16)
    back = low_dot(d_inner, in_ref[...], ((1,), (1,)))

    @pl.when(pl.program_id(0) == 0)
    def _():
        d_normed_ref[...] = back

    @pl.when(pl.program_id(0) > 0)
    def _():
        d_normed_ref[...] += back


def inner_backward(d_out, normed, slope, full_down, full_in):
    rows, width = d_out.shape
    inner = slope.shape[1]
    tile = 512
    whole = pl.BlockSpec((rows, width), lambda step: (0, 0))
    columns = pl.BlockSpec((rows, tile), lambda step: (0, step))
    return pl.pallas_call(
        inner_backward_body,
        grid=(inner // tile,),
        in_specs=[
            whole,
            whole,
            columns,
            pl.BlockSpec((tile, width), lambda step: (step, 0)),
            pl.BlockSpec((width, tile), lambda step: (0, step)),
        ],
        out_specs=[
            pl.BlockSpec((width, tile), lambda step: (0, step)),
            pl.BlockSpec((1, tile), lambda step: (0, step)),
            whole,
        ],
        out_shape=[
            jax.ShapeDtypeStruct((width, inner), jnp.bfloat16),
            jax.ShapeDtypeStruct((1, inner), jnp.float32),
            jax.ShapeDtypeStruct((rows, width), jnp.float32),
        ],
        name="inner_backward",
    )(d_out, normed, slope, full_down, full_in)


def swap_bit(count, bit):
    return [(place, place ^ (1 << bit)) for place in range(count)]


def add_up(terms):
    total = terms[0].astype(jnp.float32)
    for term in terms[1:]:
        total = total + term.astype(jnp.float32)
    return total


def reduce_stages(blocks, rep_first):
    count = lax.axis_size("fsdp")
    place = lax.axis_index("fsdp")
    replica = lax.axis_index("rep")
    cross = [(0, 1), (1, 0)]
    half = blocks.shape[-1] // 2
    terms = [blocks]
    left, bit = count, 0
    while left > 1:
        mine = (place >> bit) & 1
        paired = [term.reshape((left // 2, 2) + term.shape[1:]) for term in terms]
        away = [lax.dynamic_index_in_dim(term, 1 - mine, 1, keepdims=False) for term in paired]
        home = [lax.dynamic_index_in_dim(term, mine, 1, keepdims=False) for term in paired]
        sent = add_up(away).astype(jnp.bfloat16)
        terms = home + [lax.ppermute(sent, "fsdp", swap_bit(count, bit))]
        left, bit = left // 2, bit + 1
        if rep_first and bit == 1:
            away = [lax.dynamic_slice_in_dim(term, (1 - replica) * half, half, 2) for term in terms]
            home = [lax.dynamic_slice_in_dim(term, replica * half, half, 2) for term in terms]
            sent = add_up(away).astype(jnp.bfloat16)
            terms = home + [lax.ppermute(sent, "rep", cross)]
    low = add_up(terms)[0].astype(jnp.bfloat16)
    if lax.axis_size("rep") != 2:
        return lax.psum(low, "rep").astype(jnp.float32)
    other = lax.ppermute(low, "rep", cross)
    if not rep_first:
        return low.astype(jnp.float32) + other.astype(jnp.float32)
    pair = [jnp.where(replica == 0, low, other), jnp.where(replica == 0, other, low)]
    return jnp.concatenate(pair, axis=-1).astype(jnp.float32)


def reduce_matrix(grad, rep_first=False):
    count = lax.axis_size("fsdp")
    blocks = grad.astype(jnp.bfloat16).reshape(count, grad.shape[0] // count, grad.shape[1])
    return reduce_stages(blocks, rep_first and lax.axis_size("rep") == 2)


def reduce_small(time_w2_grad, parts):
    count = lax.axis_size("fsdp")
    width = time_w2_grad.shape[1]
    big = time_w2_grad.astype(jnp.bfloat16).reshape(count, -1, width)
    flat = jnp.concatenate([part.astype(jnp.bfloat16) for part in parts], axis=1)
    sizes = [part.shape[1] for part in parts]
    used = sum(sizes)
    rows = -(-used // width)
    flat = jnp.pad(flat, ((0, 0), (0, rows * width - used))).reshape(count, rows, width)
    summed = reduce_stages(jnp.concatenate([big, flat], axis=1), False)
    own_big = summed[: big.shape[1]]
    own_flat = summed[big.shape[1] :].reshape(-1)
    pieces, start = [], 0
    for size in sizes:
        pieces.append(own_flat[start : start + size])
        start += size
    return own_big, pieces


def gather_blocks(shards):
    count = lax.axis_size("fsdp")
    place = lax.axis_index("fsdp")
    held = jnp.concatenate(shards, axis=1)[None]
    whole = []
    for bit in reversed(range(count.bit_length() - 1)):
        other = lax.ppermute(held, "fsdp", swap_bit(count, bit))
        upper = ((place >> bit) & 1) == 1
        widths = [shard.shape[1] for shard in shards] if bit == 0 else [held.shape[-1]]
        start, joined = 0, []
        for width in widths:
            one = held[..., start : start + width]
            two = other[..., start : start + width]
            pair = [jnp.where(upper, two, one), jnp.where(upper, one, two)]
            shape = (2 * held.shape[0], held.shape[1], width)
            joined.append(jnp.stack(pair, axis=1).reshape(shape))
            start += width
        held, whole = joined[0], joined
    return whole


def gather_small(time_w2, parts):
    count = lax.axis_size("fsdp")
    width = time_w2.shape[1]
    flat = jnp.concatenate([part.reshape(-1) for part in parts])
    rows = -(-flat.shape[0] // width)
    flat = jnp.pad(flat, (0, rows * width - flat.shape[0])).reshape(rows, width)
    (whole,) = gather_blocks([jnp.concatenate([time_w2, flat], axis=0)])
    full_tw2 = whole[:, : time_w2.shape[0]].reshape(-1, width)
    flat = whole[:, time_w2.shape[0] :].reshape(count, -1)
    pieces, start = [], 0
    for part in parts:
        pieces.append(flat[:, start : start + part.size].reshape((count,) + part.shape))
        start += part.size
    return full_tw2, pieces


def per_device(
    tokens,
    timesteps,
    split_at,
    sample_weight,
    cotangent,
    time_w1,
    time_w2,
    attn_qkv,
    attn_out,
    ff_in,
    ff_out,
    biases,
    norm_gains,
    ff_bias,
    time_bias,
):
    seqs, length, width = tokens.shape
    width_in = attn_qkv.shape[1]
    full_tw2, pieces = gather_small(time_w2, [time_w1, biases, norm_gains, ff_bias, time_bias])
    full_tw1 = pieces[0].reshape(-1, time_w1.shape[1])
    full_bias = pieces[1].swapaxes(0, 1).reshape(biases.shape[0], -1)
    full_gain = pieces[2].swapaxes(0, 1).reshape(norm_gains.shape[0], -1)
    full_ffb = pieces[3].reshape(-1)
    full_tb = pieces[4].reshape(-1)
    (full_qkv,) = gather_blocks([attn_qkv])
    full_qkv = full_qkv.reshape(-1, width_in)
    full_out, full_in = gather_blocks([attn_out, ff_in])
    full_out = full_out.reshape(-1, attn_out.shape[1])
    full_in = full_in.reshape(-1, ff_in.shape[1])
    (full_down,) = gather_blocks([ff_out])
    full_down = full_down.reshape(-1, ff_out.shape[1])
    bias_rows = full_bias.astype(jnp.float32)
    gain_rows = full_gain.astype(jnp.float32)
    sinus = sinusoid(timesteps, full_tw1.shape[0])
    pre_time = precise(sinus, full_tw1.astype(jnp.float32)) + full_tb.astype(jnp.float32)
    hidden_time, silu_pull = jax.vjp(jax.nn.silu, pre_time)
    temb = precise(hidden_time, full_tw2.astype(jnp.float32)) + bias_rows[0]
    token_rows = (tokens.astype(jnp.float32) + temb[:, None, :]).reshape(seqs * length, width)
    rows_low = token_rows.astype(jnp.bfloat16)
    qkv_bias = jnp.concatenate([bias_rows[1], jnp.zeros((width,), jnp.float32), bias_rows[2]])
    projected = jnp.dot(rows_low, full_qkv, preferred_element_type=jnp.float32) + qkv_bias
    projected = projected.astype(jnp.bfloat16)
    context_low, attend = attend_forward(projected, length)
    resid_attn = (
        token_rows
        + jnp.dot(context_low, full_out, preferred_element_type=jnp.float32)
        + bias_rows[3]
    )
    normed, first_pull = jax.vjp(normalize, resid_attn, gain_rows[0], bias_rows[4])
    normed_low = normed.astype(jnp.bfloat16)
    ff_inner = jnp.dot(normed_low, full_in, preferred_element_type=jnp.float32) + full_ffb.astype(
        jnp.float32
    )
    twice_cdf = 1.0 + lax.erf(ff_inner * math.sqrt(0.5))
    active_low = (0.5 * ff_inner * twice_cdf).astype(jnp.bfloat16)
    density = jnp.exp(-0.5 * ff_inner * ff_inner) * (1.0 / math.sqrt(2.0 * math.pi))
    slope_low = (0.5 * twice_cdf + ff_inner * density).astype(jnp.bfloat16)
    resid_ff = (
        normed + jnp.dot(active_low, full_down, preferred_element_type=jnp.float32) + bias_rows[5]
    )
    output, second_pull = jax.vjp(normalize, resid_ff, gain_rows[1], bias_rows[6])
    positions = lax.iota(jnp.int32, length)
    target_mask = (positions[None, :] >= split_at[:, None]).astype(jnp.float32)
    grad_out = (
        cotangent.astype(jnp.float32) * (sample_weight[:, None] * target_mask)[:, :, None]
    ).reshape(seqs * length, width)
    d_ff, d_gain_two, d_shift_two = second_pull(grad_out)
    d_ffout_bias = jnp.sum(d_ff, axis=0)
    d_ff_low = d_ff.astype(jnp.bfloat16)
    grad_down = contract_rows(active_low, d_ff_low)
    grad_in, d_ff_bias, back = inner_backward(d_ff_low, normed_low, slope_low, full_down, full_in)
    d_attn, d_gain_one, d_shift_one = first_pull(d_ff + back)
    d_out_bias = jnp.sum(d_attn, axis=0)
    d_attn_low = d_attn.astype(jnp.bfloat16)
    grad_out_proj = contract_rows(context_low, d_attn_low)
    d_context = times_transpose(d_attn_low, full_out).astype(jnp.bfloat16)
    d_projected_low, bias_sums = attend_backward(projected, attend, d_context, length)
    bias_sums = jnp.sum(bias_sums, axis=0)
    d_query_bias, d_value_bias = bias_sums[0], bias_sums[1]
    grad_qkv = contract_rows(rows_low, d_projected_low)
    d_rows = d_attn + times_transpose(d_projected_low, full_qkv)
    d_rows_seq = d_rows.reshape(seqs, length, width)
    d_temb = jnp.sum(d_rows_seq, axis=1)
    d_temb_bias = jnp.sum(d_temb, axis=0)
    grad_tw2 = precise(hidden_time.T, d_temb)
    d_hidden_time = precise(d_temb, full_tw2.astype(jnp.float32).T)
    (d_pre_time,) = silu_pull(d_hidden_time)
    d_time_bias = jnp.sum(d_pre_time, axis=0)
    grad_tw1 = precise(sinus.T, d_pre_time)
    grad_bias_rows = jnp.stack(
        [
            d_temb_bias,
            d_query_bias,
            d_value_bias,
            d_out_bias,
            d_shift_one,
            d_ffout_bias,
            d_shift_two,
        ]
    )
    grad_gain_rows = jnp.stack([d_gain_one, d_gain_two])
    count = lax.axis_size("fsdp")

    def by_column(rows_in):
        rows_n, cols_n = rows_in.shape
        return rows_in.reshape(rows_n, count, cols_n // count).swapaxes(0, 1).reshape(count, -1)

    share_down = reduce_matrix(grad_down)
    mid_width = grad_in.shape[1]
    share_mid = reduce_matrix(jnp.concatenate([grad_in, grad_out_proj], axis=1))
    share_in, share_out = share_mid[:, :mid_width], share_mid[:, mid_width:]
    share_qkv = reduce_matrix(grad_qkv, rep_first=True)
    share_tw2, pieces = reduce_small(
        grad_tw2,
        [
            grad_tw1.reshape(count, -1),
            by_column(grad_bias_rows),
            by_column(grad_gain_rows),
            d_ff_bias.reshape(count, -1),
            d_time_bias.reshape(count, -1),
        ],
    )
    summed = (
        pieces[0].reshape(time_w1.shape),
        share_tw2,
        share_qkv,
        share_out,
        share_in,
        share_down,
        pieces[1].reshape(biases.shape),
        pieces[2].reshape(norm_gains.shape),
        pieces[3],
        pieces[4],
    )
    output_low = output.reshape(seqs, length, width).astype(jnp.bfloat16)
    grad_tokens = d_rows_seq.astype(jnp.bfloat16)
    return (
        output_low,
        grad_tokens,
        summed[0],
        summed[1],
        summed[2],
        summed[3],
        summed[4],
        summed[5],
        summed[6],
        summed[7],
        summed[8],
        summed[9],
    )


def solution(mesh):
    placed = (
        P(("rep", "fsdp"), None, None),
        P(("rep", "fsdp")),
        P(("rep", "fsdp")),
        P(("rep", "fsdp")),
        P(("rep", "fsdp"), None, None),
        P("fsdp", None),
        P("fsdp", None),
        P("fsdp", None),
        P("fsdp", None),
        P("fsdp", None),
        P("fsdp", None),
        P(None, "fsdp"),
        P(None, "fsdp"),
        P("fsdp"),
        P("fsdp"),
    )
    return jax.shard_map(
        per_device,
        mesh=mesh,
        in_specs=placed,
        out_specs=(
            P(("rep", "fsdp"), None, None),
            P(("rep", "fsdp"), None, None),
            P("fsdp", None),
            P("fsdp", None),
            P("fsdp", None),
            P("fsdp", None),
            P("fsdp", None),
            P("fsdp", None),
            P(None, "fsdp"),
            P(None, "fsdp"),
            P("fsdp"),
            P("fsdp"),
        ),
        check_vma=False,
    )
```
